1024 devices in a mesh: tensor: 32 (over y, z_hi, core), context: 32 (over z_lo, x).
Axes of the slice: x: 4, y: 4, z: 32 (z_hi: 4, z_lo: 8; z = z_hi * 8 + z_lo), core: 2. Of those that a mesh axis runs over, the one named last changes fastest.
Arguments:
- queries: bfloat16 [8192, 4096], P('tensor', 'context'), parts along dimension 0, may hold values from -6 to 6
- keys: bfloat16 [8192, 4096], P('tensor', 'context'), parts along dimension 0, may hold values from -6 to 6
- values: bfloat16 [8192, 4096], P('tensor', 'context'), parts along dimension 0, may hold values from -6 to 6
- filters: float32 [8192, 4096], P(('tensor', 'context')), parts along dimension 0, may hold values from -1 to 1
- skip: float32 [8192], P('tensor'), parts along dimension 0, may hold values from -3 to 3
Outputs:
- output: bfloat16 [8192, 4096], P('tensor', 'context'), parts along dimension 0
The draws below stay inside these ranges and needn't reach their ends.
There are 32 independent parts, one for each index of `tensor`. The reference program is written for one: setup_inputs(seed, part) draws one part's arguments, and reference() takes and returns one part's arrays. A program takes and returns all parts, laid end to end along the dimension named above; each array names one. Nothing has to cross between parts.
All inputs are finite; a program needn't handle non-finite values.
Results may differ from the reference program's by a relative error of at most 0.008.
Values may be sent and summed in bfloat16 or wider, within the bound.
A program may use at most 32 MiB of HBM per device.

```python
import jax
import jax.numpy as jnp

C = 256
SEQ = 4096


def draw_filters(key, part):
    key_rate, key_noise = jax.random.split(jax.random.fold_in(key, 17), 2)
    lowest, highest = (0.5 / SEQ, 1.0 / 30.0)
    rates = jnp.exp(jax.random.uniform(key_rate, (C, 1), jnp.float32, jnp.log(lowest), jnp.log(highest)))
    amplitude = jnp.sqrt(1.0 - jnp.exp(-2.0 * rates))
    times = jnp.arange(SEQ, dtype=jnp.float32)[None, :]
    envelope = jnp.exp(-rates * times)
    noise = jnp.clip(jax.random.normal(key_noise, (C, SEQ), jnp.float32), -3.5, 3.5)
    return amplitude * noise * envelope


def level_of(stream_key, shape, shards, smallest, largest):
    loudness, own = 1.0, jax.random.fold_in(stream_key, 6)
    for position, shards_of in shards:
        heights = jnp.exp(jax.random.uniform(jax.random.fold_in(own, position), (shards_of,), jnp.float32, smallest / len(shards), largest / len(shards)))
        loudness = loudness * jnp.repeat(heights, shape[position] // shards_of).reshape([-1 if axis == position else 1 for axis in range(len(shape))])
    return loudness


def normal_values(own_key, extent, width, bound, cuts=(), kind=jnp.bfloat16):
    level = level_of(own_key, extent, cuts, -0.22, 0.18) if cuts else 1.0
    values = jax.random.normal(own_key, extent, jnp.float32) * width * level
    return jnp.minimum(jnp.maximum(values, -bound), bound).astype(kind)


def setup_inputs(seed: int = 0, part: int = 0) -> dict:
    key_list = jax.random.split(jax.random.key(seed), 6)
    part_splits = jax.random.split(jax.random.fold_in(key_list[5], part), 6)
    return {
        "queries": normal_values(part_splits[0], (C, SEQ), 1.0, 6.0, ((1, 32),)),
        "keys": normal_values(part_splits[1], (C, SEQ), 1.0, 6.0, ((1, 32),)),
        "values": normal_values(part_splits[2], (C, SEQ), 1.0, 6.0, ((1, 32),)),
        "filters": draw_filters(jax.random.fold_in(jax.random.fold_in(key_list[5], part), 71), part),
        "skip": normal_values(part_splits[4], (C,), 0.5, 3.0, (), jnp.float32),
    }


def reference(queries, keys, values, filters, skip):
    gated = (keys.astype(jnp.float32) * values.astype(jnp.float32)).astype(jnp.bfloat16)
    padded_len = 2 * SEQ
    spectrum = jnp.fft.rfft(gated.astype(jnp.float32), n=padded_len, axis=1) * jnp.fft.rfft(filters, n=padded_len, axis=1)
    convolved = jnp.fft.irfft(spectrum, n=padded_len, axis=1)[:, :SEQ].astype(jnp.bfloat16)
    output = queries.astype(jnp.float32) * (convolved.astype(jnp.float32) + skip[:, None] * gated.astype(jnp.float32))
    return output.astype(jnp.bfloat16)
```

```python
import functools

import jax
import jax.numpy as jnp
from jax import lax
from jax.experimental import pallas as pl
from jax.experimental.pallas import tpu as pltpu
from jax.sharding import PartitionSpec as P

MESH = pl.DeviceIdType.MESH
EARLY = 3


def conv_kernel(
    keys_hbm,
    values_hbm,
    filters_hbm,
    conv_ref,
    gated_ref,
    keys_ref,
    values_ref,
    taps_ref,
    toep_ref,
    arrived_ref,
    padded_ref,
    mixed_ref,
    outgoing_ref,
    load_sem,
    send_sem,
    recv_sem,
    back_send_sem,
    back_recv_sem,
):
    shards, local_ch, block = gated_ref.shape
    me = lax.axis_index("context")
    tensor = lax.axis_index("tensor")
    barrier = pltpu.get_barrier_semaphore()

    def greet(k, carry):
        peer = lax.rem(me + k, shards)
        pl.semaphore_signal(barrier, inc=1, device_id=(tensor, peer), device_id_type=MESH)
        return carry

    lax.fori_loop(1, shards, greet, 0)

    key_load = pltpu.make_async_copy(keys_hbm, keys_ref, load_sem.at[0])
    value_load = pltpu.make_async_copy(values_hbm, values_ref, load_sem.at[1])
    tap_load = pltpu.make_async_copy(filters_hbm, taps_ref, load_sem.at[2])
    key_load.start()
    value_load.start()
    tap_load.start()
    padded_ref[pl.ds(0, (shards - 1) * local_ch), :] = jnp.zeros(
        ((shards - 1) * local_ch, block), jnp.float32
    )
    key_load.wait()
    value_load.wait()
    gated_ref[...] = (
        keys_ref[...].astype(jnp.float32) * values_ref[...].astype(jnp.float32)
    ).astype(jnp.bfloat16)
    tap_load.wait()

    row_ids = lax.broadcasted_iota(jnp.int32, (block, block), 0)
    col_ids = lax.broadcasted_iota(jnp.int32, (block, block), 1)
    same_block = col_ids >= row_ids

    def build(c):
        def step(d, before):
            start = pl.multiple_of(d * block, block)
            row = taps_ref[c : c + 1, pl.ds(start, block)]
            turned = pltpu.roll(
                jnp.broadcast_to(row, (block, block)), 0, 1, stride=1, stride_axis=0
            )
            toep_ref[c, pl.ds(start, block), :] = jnp.where(same_block, turned, before).astype(
                jnp.bfloat16
            )
            return turned

        lax.fori_loop(0, shards, step, jnp.zeros((block, block), jnp.float32))

    for c in range(EARLY):
        build(c)
    pl.semaphore_wait(barrier, shards - 1)

    def send_out(k, carry):
        peer = lax.rem(me + k, shards)
        pltpu.make_async_remote_copy(
            src_ref=gated_ref.at[peer],
            dst_ref=arrived_ref.at[me],
            send_sem=send_sem,
            recv_sem=recv_sem,
            device_id=(tensor, peer),
            device_id_type=MESH,
        ).start()
        return carry

    lax.fori_loop(1, shards, send_out, 0)
    own = pltpu.make_async_copy(gated_ref.at[me], arrived_ref.at[me], recv_sem)
    own.start()
    for c in range(EARLY, local_ch):
        build(c)
    pltpu.make_async_copy(arrived_ref, arrived_ref, recv_sem).wait()

    padded_ref[pl.ds((shards - 1) * local_ch, shards * local_ch), :] = (
        arrived_ref[...].astype(jnp.float32).reshape(shards * local_ch, block)
    )

    for c in range(local_ch):
        shifted = jnp.concatenate(
            [
                padded_ref[pl.ds((shards - 1 - d) * local_ch + c, shards, stride=local_ch), :]
                for d in range(shards)
            ],
            axis=1,
        ).astype(jnp.bfloat16)
        mixed_ref[pl.ds(c, shards, stride=local_ch), :] = jnp.dot(
            shifted, toep_ref[c], preferred_element_type=jnp.float32
        )
    outgoing_ref[...] = (
        mixed_ref[...].reshape(shards, local_ch, block).astype(jnp.bfloat16)
    )

    def send_back(k, carry):
        peer = lax.rem(me + k, shards)
        pltpu.make_async_remote_copy(
            src_ref=outgoing_ref.at[peer],
            dst_ref=conv_ref.at[me],
            send_sem=back_send_sem,
            recv_sem=back_recv_sem,
            device_id=(tensor, peer),
            device_id_type=MESH,
        ).start()
        return carry

    lax.fori_loop(1, shards, send_back, 0)
    own_back = pltpu.make_async_copy(outgoing_ref.at[me], conv_ref.at[me], back_recv_sem)
    own_back.start()
    others = arrived_ref.at[pl.ds(0, shards - 1)]
    pltpu.make_async_copy(others, others, send_sem).wait()
    pltpu.make_async_copy(conv_ref, conv_ref, back_recv_sem).wait()
    pltpu.make_async_copy(others, others, back_send_sem).wait()


def per_device(queries, keys, values, filters, skip):
    channels, block = keys.shape
    shards = lax.axis_size("context")
    local_ch = channels // shards
    stacked = (shards, local_ch, block)
    vmem = pl.BlockSpec(memory_space=pltpu.VMEM)
    anywhere = pl.BlockSpec(memory_space=pltpu.HBM)
    conv, gated = pl.pallas_call(
        conv_kernel,
        out_shape=(
            jax.ShapeDtypeStruct(stacked, jnp.bfloat16),
            jax.ShapeDtypeStruct(stacked, jnp.bfloat16),
        ),
        in_specs=[anywhere] * 3,
        out_specs=(vmem, vmem),
        scratch_shapes=[
            pltpu.VMEM(stacked, jnp.bfloat16),
            pltpu.VMEM(stacked, jnp.bfloat16),
            pltpu.VMEM((local_ch, shards * block), jnp.float32),
            pltpu.VMEM((local_ch, shards * block, block), jnp.bfloat16),
            pltpu.VMEM(stacked, jnp.bfloat16),
            pltpu.VMEM(((2 * shards - 1) * local_ch, block), jnp.float32),
            pltpu.VMEM((shards * local_ch, block), jnp.float32),
            pltpu.VMEM(stacked, jnp.bfloat16),
            pltpu.SemaphoreType.DMA((3,)),
            pltpu.SemaphoreType.DMA,
            pltpu.SemaphoreType.DMA,
            pltpu.SemaphoreType.DMA,
            pltpu.SemaphoreType.DMA,
        ],
        compiler_params=pltpu.CompilerParams(
            collective_id=0, has_side_effects=True, vmem_limit_bytes=66500000
        ),
        name="hyena_conv",
    )(keys.reshape(stacked), values.reshape(stacked), filters)
    result = queries.astype(jnp.float32) * (
        conv.reshape(channels, block).astype(jnp.float32)
        + skip[:, None] * gated.reshape(channels, block).astype(jnp.float32)
    )
    return result.astype(jnp.bfloat16)


def solution(mesh):
    placed = (
        P("tensor", "context"),
        P("tensor", "context"),
        P("tensor", "context"),
        P(("tensor", "context"), None),
        P("tensor"),
    )
    return jax.shard_map(
        per_device, mesh=mesh, in_specs=placed, out_specs=P("tensor", "context"), check_vma=False
    )
```

```python
import functools

import jax
import jax.numpy as jnp
from jax import lax
from jax.experimental import pallas as pl
from jax.experimental.pallas import tpu as pltpu
from jax.sharding import PartitionSpec as P

MESH = pl.DeviceIdType.MESH
EARLY = 4


def conv_kernel(
    keys_hbm,
    values_hbm,
    filters_hbm,
    skip_hbm,
    conv_ref,
    skipped_ref,
    gated_ref,
    skip_ref,
    keys_ref,
    values_ref,
    taps_ref,
    toep_ref,
    arrived_ref,
    padded_ref,
    mixed_ref,
    outgoing_ref,
    load_sem,
    send_sem,
    recv_sem,
    back_send_sem,
    back_recv_sem,
):
    shards, local_ch, block = gated_ref.shape
    me = lax.axis_index("context")
    tensor = lax.axis_index("tensor")
    upper = me // (shards // 2)
    barrier = pltpu.get_barrier_semaphore()

    def greet(k, carry):
        peer = lax.rem(me + k, shards)
        pl.semaphore_signal(barrier, inc=1, device_id=(tensor, peer), device_id_type=MESH)
        return carry

    lax.fori_loop(1, shards, greet, 0)

    key_load = pltpu.make_async_copy(keys_hbm, keys_ref, load_sem.at[0])
    value_load = pltpu.make_async_copy(values_hbm, values_ref, load_sem.at[1])
    tap_load = pltpu.make_async_copy(filters_hbm, taps_ref, load_sem.at[2])
    key_load.start()
    value_load.start()
    tap_load.start()
    skip_load = pltpu.make_async_copy(skip_hbm, skip_ref, load_sem.at[3])
    skip_load.start()
    padded_ref[pl.ds(0, (shards - 1) * local_ch), :] = jnp.zeros(
        ((shards - 1) * local_ch, block), jnp.float32
    )
    key_load.wait()
    value_load.wait()
    gated_ref[...] = (
        keys_ref[...].astype(jnp.float32) * values_ref[...].astype(jnp.float32)
    ).astype(jnp.bfloat16)
    tap_load.wait()

    row_ids = lax.broadcasted_iota(jnp.int32, (block, block), 0)
    col_ids = lax.broadcasted_iota(jnp.int32, (block, block), 1)
    same_block = col_ids >= row_ids

    def build(c):
        before = jnp.zeros((block, block), jnp.float32)
        for d in range(shards):
            row = taps_ref[c : c + 1, d * block : (d + 1) * block]
            turned = pltpu.roll(
                jnp.broadcast_to(row, (block, block)), 0, 1, stride=1, stride_axis=0
            )
            toep_ref[c, d * block : (d + 1) * block, :] = jnp.where(
                same_block, turned, before
            ).astype(jnp.bfloat16)
            before = turned

    for c in range(EARLY):
        build(c)
    pl.semaphore_wait(barrier, shards - 1)

    def send_out(k, carry):
        peer = upper * k + (1 - upper) * (shards - 1 - k)

        @pl.when(peer != me)
        def _():
            pltpu.make_async_remote_copy(
                src_ref=gated_ref.at[peer],
                dst_ref=arrived_ref.at[me],
                send_sem=send_sem,
                recv_sem=recv_sem,
                device_id=(tensor, peer),
                device_id_type=MESH,
            ).start()
        return carry

    lax.fori_loop(0, shards, send_out, 0)
    own = pltpu.make_async_copy(gated_ref.at[me], arrived_ref.at[me], recv_sem)
    own.start()
    for c in range(EARLY, local_ch):
        build(c)
    pltpu.make_async_copy(arrived_ref, arrived_ref, recv_sem).wait()

    padded_ref[pl.ds((shards - 1) * local_ch, shards * local_ch), :] = (
        arrived_ref[...].astype(jnp.float32).reshape(shards * local_ch, block)
    )

    for c in range(local_ch):
        shifted = jnp.concatenate(
            [
                padded_ref[pl.ds((shards - 1 - d) * local_ch + c, shards, stride=local_ch), :]
                for d in range(shards)
            ],
            axis=1,
        ).astype(jnp.bfloat16)
        mixed_ref[pl.ds(c, shards, stride=local_ch), :] = jnp.dot(
            shifted, toep_ref[c], preferred_element_type=jnp.float32
        )
    outgoing_ref[...] = (
        mixed_ref[...].reshape(shards, local_ch, block).astype(jnp.bfloat16)
    )

    def send_back(k, carry):
        peer = upper * k + (1 - upper) * (shards - 1 - k)

        @pl.when(peer != me)
        def _():
            pltpu.make_async_remote_copy(
                src_ref=outgoing_ref.at[peer],
                dst_ref=conv_ref.at[me],
                send_sem=back_send_sem,
                recv_sem=back_recv_sem,
                device_id=(tensor, peer),
                device_id_type=MESH,
            ).start()
        return carry

    lax.fori_loop(0, shards, send_back, 0)
    own_back = pltpu.make_async_copy(outgoing_ref.at[me], conv_ref.at[me], back_recv_sem)
    own_back.start()
    others = arrived_ref.at[pl.ds(0, shards - 1)]
    skip_load.wait()
    columns = jnp.broadcast_to(skip_ref[...][None, :], (block, shards * local_ch)).T
    skipped_ref[...] = columns * gated_ref[...].astype(jnp.float32).reshape(
        shards * local_ch, block
    )
    pltpu.make_async_copy(others, others, send_sem).wait()
    pltpu.make_async_copy(conv_ref, conv_ref, back_recv_sem).wait()
    pltpu.make_async_copy(others, others, back_send_sem).wait()


def in_hbm(array):
    return pltpu.with_memory_space_constraint(array, pltpu.HBM)


def per_device(queries, keys, values, filters, skip):
    channels, block = keys.shape
    shards = lax.axis_size("context")
    local_ch = channels // shards
    stacked = (shards, local_ch, block)
    vmem = pl.BlockSpec(memory_space=pltpu.VMEM)
    anywhere = pl.BlockSpec(memory_space=pltpu.HBM)
    conv, skipped = pl.pallas_call(
        conv_kernel,
        out_shape=(
            jax.ShapeDtypeStruct(stacked, jnp.bfloat16),
            jax.ShapeDtypeStruct((channels, block), jnp.float32),
        ),
        in_specs=[anywhere] * 4,
        out_specs=(vmem, vmem),
        scratch_shapes=[
            pltpu.VMEM(stacked, jnp.bfloat16),
            pltpu.VMEM((channels,), jnp.float32),
            pltpu.VMEM(stacked, jnp.bfloat16),
            pltpu.VMEM(stacked, jnp.bfloat16),
            pltpu.VMEM((local_ch, shards * block), jnp.float32),
            pltpu.VMEM((local_ch, shards * block, block), jnp.bfloat16),
            pltpu.VMEM(stacked, jnp.bfloat16),
            pltpu.VMEM(((2 * shards - 1) * local_ch, block), jnp.float32),
            pltpu.VMEM((shards * local_ch, block), jnp.float32),
            pltpu.VMEM(stacked, jnp.bfloat16),
            pltpu.SemaphoreType.DMA((4,)),
            pltpu.SemaphoreType.DMA,
            pltpu.SemaphoreType.DMA,
            pltpu.SemaphoreType.DMA,
            pltpu.SemaphoreType.DMA,
        ],
        compiler_params=pltpu.CompilerParams(
            collective_id=0, has_side_effects=True, vmem_limit_bytes=40 << 20
        ),
        name="hyena_conv",
    )(*(in_hbm(x) for x in (keys.reshape(stacked), values.reshape(stacked), filters, skip)))
    result = queries.astype(jnp.float32) * (
        conv.reshape(channels, block).astype(jnp.float32) + skipped
    )
    return result.astype(jnp.bfloat16)


def solution(mesh):
    placed = (
        P("tensor", "context"),
        P("tensor", "context"),
        P("tensor", "context"),
        P(("tensor", "context"), None),
        P("tensor"),
    )
    return jax.shard_map(
        per_device, mesh=mesh, in_specs=placed, out_specs=P("tensor", "context"), check_vma=False
    )
```

```python
import functools

import jax
import jax.numpy as jnp
from jax import lax
from jax.experimental import pallas as pl
from jax.experimental.pallas import tpu as pltpu
from jax.sharding import PartitionSpec as P

MESH = pl.DeviceIdType.MESH
EARLY = 2
FIRST = 8
SECOND = 16


def conv_kernel(
    keys_hbm,
    values_hbm,
    filters_hbm,
    skip_hbm,
    conv_ref,
    skipped_ref,
    gated_ref,
    skip_ref,
    keys_ref,
    values_ref,
    taps_ref,
    toep_ref,
    arrived_ref,
    padded_ref,
    mixed_ref,
    outgoing_ref,
    load_sem,
    send_sem,
    recv_sem,
    back_send_sem,
    back_recv_sem,
):
    shards, local_ch, block = gated_ref.shape
    me = lax.axis_index("context")
    tensor = lax.axis_index("tensor")
    upper = me // (shards // 2)
    barrier = pltpu.get_barrier_semaphore()

    def greet(k, carry):
        peer = lax.rem(me + k, shards)
        pl.semaphore_signal(barrier, inc=1, device_id=(tensor, peer), device_id_type=MESH)
        return carry

    lax.fori_loop(1, shards, greet, 0)

    key_load = pltpu.make_async_copy(keys_hbm, keys_ref, load_sem.at[0])
    value_load = pltpu.make_async_copy(values_hbm, values_ref, load_sem.at[1])
    tap_load = pltpu.make_async_copy(filters_hbm, taps_ref, load_sem.at[2])
    key_load.start()
    value_load.start()
    tap_load.start()
    skip_load = pltpu.make_async_copy(skip_hbm, skip_ref, load_sem.at[3])
    skip_load.start()
    padded_ref[pl.ds(0, (shards - 1) * local_ch), :] = jnp.zeros(
        ((shards - 1) * local_ch, block), jnp.float32
    )
    key_load.wait()
    value_load.wait()
    gated_ref[...] = (
        keys_ref[...].astype(jnp.float32) * values_ref[...].astype(jnp.float32)
    ).astype(jnp.bfloat16)
    tap_load.wait()

    row_ids = lax.broadcasted_iota(jnp.int32, (block, block), 0)
    col_ids = lax.broadcasted_iota(jnp.int32, (block, block), 1)
    same_block = col_ids >= row_ids

    def build(c):
        before = jnp.zeros((block, block), jnp.float32)
        for d in range(shards):
            row = taps_ref[c : c + 1, d * block : (d + 1) * block]
            turned = pltpu.roll(
                jnp.broadcast_to(row, (block, block)), 0, 1, stride=1, stride_axis=0
            )
            toep_ref[c, d * block : (d + 1) * block, :] = jnp.where(
                same_block, turned, before
            ).astype(jnp.bfloat16)
            before = turned

    for c in range(EARLY):
        build(c)
    pl.semaphore_wait(barrier, shards - 1)
    mine = recv_sem.at[lax.min(me // FIRST, 2)]

    def send_out(k, carry):
        peer = upper * k + (1 - upper) * (shards - 1 - k)

        @pl.when(peer != me)
        def _():
            pltpu.make_async_remote_copy(
                src_ref=gated_ref.at[peer],
                dst_ref=arrived_ref.at[me],
                send_sem=send_sem,
                recv_sem=mine,
                device_id=(tensor, peer),
                device_id_type=MESH,
            ).start()

        return carry

    lax.fori_loop(0, shards, send_out, 0)
    pltpu.make_async_copy(gated_ref.at[me], arrived_ref.at[me], mine).start()
    for c in range(EARLY, local_ch):
        build(c)

    def send_back(peer):
        @pl.when(peer != me)
        def _():
            pltpu.make_async_remote_copy(
                src_ref=outgoing_ref.at[peer],
                dst_ref=conv_ref.at[me],
                send_sem=back_send_sem,
                recv_sem=back_recv_sem,
                device_id=(tensor, peer),
                device_id_type=MESH,
            ).start()

    for group, (low, high) in enumerate(((0, FIRST), (FIRST, SECOND), (SECOND, shards))):
        part = arrived_ref.at[low:high]
        pltpu.make_async_copy(part, part, recv_sem.at[group]).wait()
        padded_ref[(shards - 1 + low) * local_ch : (shards - 1 + high) * local_ch, :] = (
            part[...].astype(jnp.float32).reshape((high - low) * local_ch, block)
        )
        for c in range(local_ch):
            shifted = jnp.concatenate(
                [
                    padded_ref[
                        pl.ds((shards - 1 + low - d) * local_ch + c, high - low, stride=local_ch), :
                    ]
                    for d in range(high)
                ],
                axis=1,
            ).astype(jnp.bfloat16)
            mixed_ref[pl.ds(low * local_ch + c, high - low, stride=local_ch), :] = jnp.dot(
                shifted, toep_ref[c, : high * block, :], preferred_element_type=jnp.float32
            )
        outgoing_ref[low:high] = (
            mixed_ref[low * local_ch : high * local_ch, :]
            .reshape(high - low, local_ch, block)
            .astype(jnp.bfloat16)
        )

        def send_part(k, carry, low=low, high=high):
            send_back(upper * (low + k) + (1 - upper) * (high - 1 - k))
            return carry

        lax.fori_loop(0, high - low, send_part, 0)

    pltpu.make_async_copy(outgoing_ref.at[me], conv_ref.at[me], back_recv_sem).start()
    others = arrived_ref.at[pl.ds(0, shards - 1)]
    skip_load.wait()
    columns = jnp.broadcast_to(skip_ref[...][None, :], (block, shards * local_ch)).T
    skipped_ref[...] = columns * gated_ref[...].astype(jnp.float32).reshape(
        shards * local_ch, block
    )
    pltpu.make_async_copy(others, others, send_sem).wait()
    pltpu.make_async_copy(conv_ref, conv_ref, back_recv_sem).wait()
    pltpu.make_async_copy(others, others, back_send_sem).wait()


def in_hbm(array):
    return pltpu.with_memory_space_constraint(array, pltpu.HBM)


def per_device(queries, keys, values, filters, skip):
    channels, block = keys.shape
    shards = lax.axis_size("context")
    local_ch = channels // shards
    stacked = (shards, local_ch, block)
    vmem = pl.BlockSpec(memory_space=pltpu.VMEM)
    anywhere = pl.BlockSpec(memory_space=pltpu.HBM)
    conv, skipped = pl.pallas_call(
        conv_kernel,
        out_shape=(
            jax.ShapeDtypeStruct(stacked, jnp.bfloat16),
            jax.ShapeDtypeStruct((channels, block), jnp.float32),
        ),
        in_specs=[anywhere] * 4,
        out_specs=(vmem, vmem),
        scratch_shapes=[
            pltpu.VMEM(stacked, jnp.bfloat16),
            pltpu.VMEM((channels,), jnp.float32),
            pltpu.VMEM(stacked, jnp.bfloat16),
            pltpu.VMEM(stacked, jnp.bfloat16),
            pltpu.VMEM((local_ch, shards * block), jnp.float32),
            pltpu.VMEM((local_ch, shards * block, block), jnp.bfloat16),
            pltpu.VMEM(stacked, jnp.bfloat16),
            pltpu.VMEM(((2 * shards - 1) * local_ch, block), jnp.float32),
            pltpu.VMEM((shards * local_ch, block), jnp.float32),
            pltpu.VMEM(stacked, jnp.bfloat16),
            pltpu.SemaphoreType.DMA((4,)),
            pltpu.SemaphoreType.DMA,
            pltpu.SemaphoreType.DMA((3,)),
            pltpu.SemaphoreType.DMA,
            pltpu.SemaphoreType.DMA,
        ],
        compiler_params=pltpu.CompilerParams(
            collective_id=0, has_side_effects=True, vmem_limit_bytes=40 << 20
        ),
        name="hyena_conv",
    )(*(in_hbm(x) for x in (keys.reshape(stacked), values.reshape(stacked), filters, skip)))
    result = queries.astype(jnp.float32) * (
        conv.reshape(channels, block).astype(jnp.float32) + skipped
    )
    return result.astype(jnp.bfloat16)


def solution(mesh):
    placed = (
        P("tensor", "context"),
        P("tensor", "context"),
        P("tensor", "context"),
        P(("tensor", "context"), None),
        P("tensor"),
    )
    return jax.shard_map(
        per_device, mesh=mesh, in_specs=placed, out_specs=P("tensor", "context"), check_vma=False
    )
```

```python
import functools

import jax
import jax.numpy as jnp
from jax import lax
from jax.experimental import pallas as pl
from jax.experimental.pallas import tpu as pltpu
from jax.sharding import PartitionSpec as P

MESH = pl.DeviceIdType.MESH
FIRST = 8


def conv_kernel(
    keys_hbm,
    values_hbm,
    filters_hbm,
    skip_hbm,
    conv_ref,
    skipped_ref,
    gated_ref,
    skip_ref,
    keys_ref,
    values_ref,
    taps_ref,
    toep_ref,
    arrived_ref,
    padded_ref,
    mixed_ref,
    outgoing_ref,
    lent_ref,
    borrowed_ref,
    low_toep_ref,
    low_arrived_ref,
    low_padded_ref,
    low_mixed_ref,
    low_outgoing_ref,
    load_sem,
    send_sem,
    recv_sem,
    low_send_sem,
    low_recv_sem,
    lend_sem,
    borrow_sem,
    back_send_sem,
    low_back_send_sem,
    back_recv_sem,
    last_sem,
):
    shards, local_ch, block = gated_ref.shape
    me = lax.axis_index("context")
    tensor = lax.axis_index("tensor")
    half = shards // 2
    upper = me // half
    partner = lax.rem(me + half, shards)
    barrier = pltpu.get_barrier_semaphore()

    first_group = 1 - lax.min(tensor, 1)
    is_last = me + tensor == 0
    alone = (tensor == 0) & (partner == 0)
    borrows = (upper == 0) & (me + tensor > 0)
    lends = (upper == 1) & (partner + tensor > 0)

    def greet(k, carry):
        peer = lax.rem(me + k, shards)
        pl.semaphore_signal(barrier, inc=1, device_id=(tensor, peer), device_id_type=MESH)
        return carry

    @pl.when(jnp.logical_not(is_last))
    def _():
        lax.fori_loop(1, shards, greet, 0)

    key_load = pltpu.make_async_copy(keys_hbm, keys_ref, load_sem.at[0])
    value_load = pltpu.make_async_copy(values_hbm, values_ref, load_sem.at[1])
    tap_load = pltpu.make_async_copy(filters_hbm, taps_ref, load_sem.at[2])
    key_load.start()
    value_load.start()
    tap_load.start()
    skip_load = pltpu.make_async_copy(skip_hbm, skip_ref, load_sem.at[3])
    skip_load.start()
    padded_ref[pl.ds(0, (shards - 1) * local_ch), :] = jnp.zeros(
        ((shards - 1) * local_ch, block), jnp.float32
    )
    low_padded_ref[pl.ds(0, (half - 1) * local_ch), :] = jnp.zeros(
        ((half - 1) * local_ch, block), jnp.float32
    )
    key_load.wait()
    value_load.wait()
    gated_ref[...] = (
        keys_ref[...].astype(jnp.float32) * values_ref[...].astype(jnp.float32)
    ).astype(jnp.bfloat16)
    tap_load.wait()
    for d in range(half):
        lent_ref[d] = taps_ref[:, d * block : (d + 1) * block].astype(jnp.bfloat16)

    row_ids = lax.broadcasted_iota(jnp.int32, (block, block), 0)
    col_ids = lax.broadcasted_iota(jnp.int32, (block, block), 1)
    same_block = col_ids >= row_ids

    def turn(row):
        return pltpu.roll(jnp.broadcast_to(row, (block, block)), 0, 1, stride=1, stride_axis=0)

    def build(row_of, into, c, first, last):
        before = turn(row_of(first - 1)) if first else jnp.zeros((block, block), jnp.float32)
        for d in range(first, last):
            turned = turn(row_of(d))
            into[c, d * block : (d + 1) * block, :] = jnp.where(
                same_block, turned, before
            ).astype(jnp.bfloat16)
            before = turned

    def build_own(c):
        def row_of(d):
            return taps_ref[c : c + 1, d * block : (d + 1) * block]

        build(row_of, toep_ref, c, 0, shards)

    def build_borrowed(first, last):
        for c in range(local_ch):

            def row_of(d, c=c):
                return borrowed_ref[d].astype(jnp.float32)[c : c + 1, :]

            build(row_of, low_toep_ref, c, first, last)

    @pl.when(borrows)
    def _():
        for c in range(local_ch):
            build_own(c)

    pl.semaphore_wait(barrier, shards - 1 - first_group * lax.min(me, 1))

    @pl.when(is_last)
    def _():
        def announce(peer, carry):
            pl.semaphore_signal(last_sem, inc=1, device_id=(tensor, peer), device_id_type=MESH)
            return carry

        lax.fori_loop(1, shards, announce, 0)


    def push(source, target, sent, received, peer):
        pltpu.make_async_remote_copy(
            src_ref=source,
            dst_ref=target,
            send_sem=sent,
            recv_sem=received,
            device_id=(tensor, peer),
            device_id_type=MESH,
        ).start()

    mine = recv_sem.at[me // FIRST]
    low_mine = low_recv_sem.at[lax.rem(me, half) // FIRST]

    def send_out(peer):
        push(gated_ref.at[peer], arrived_ref.at[me], send_sem, mine, peer)

    def send_both(peer):
        push(gated_ref.at[peer + half], low_arrived_ref.at[me], low_send_sem, low_mine, peer)
        send_out(peer)

    def lend():
        push(lent_ref, borrowed_ref, lend_sem, borrow_sem, partner)

    @pl.when(upper == 0)
    def _():
        def send_low(peer, carry):
            @pl.when((peer != me) & (peer + 1 - first_group > 0))
            def _():
                send_both(peer)

            return carry

        def send_high(k, carry):
            send_out(shards - 1 - k)
            return carry

        lax.fori_loop(0, half, send_low, 0)

        @pl.when(borrows)
        def _():
            pltpu.make_async_copy(gated_ref.at[partner], low_arrived_ref.at[me], low_mine).start()

        lax.fori_loop(0, half, send_high, 0)

    @pl.when(upper == 1)
    def _():
        @pl.when(lends)
        def _():
            lend()

        def send_any(peer, carry):
            @pl.when((peer != me) & (peer + 1 - first_group > 0))
            def _():
                send_out(peer)

            return carry

        lax.fori_loop(0, shards, send_any, 0)

    pltpu.make_async_copy(gated_ref.at[me], arrived_ref.at[me], mine).start()

    @pl.when(jnp.logical_not(borrows))
    def _():
        for c in range(local_ch):
            build_own(c)

    @pl.when((tensor == 0) & (me > 0))
    def _():
        pl.semaphore_wait(last_sem, 1)
        send_out(0)

    @pl.when(borrows)
    def _():
        pltpu.make_async_copy(borrowed_ref, borrowed_ref, borrow_sem).wait()
        build_borrowed(0, half)

    def take(arrived, padded, zeros, sem, low, high):
        part = arrived.at[low:high]
        pltpu.make_async_copy(part, part, sem).wait()
        padded[(zeros + low) * local_ch : (zeros + high) * local_ch, :] = (
            part[...].astype(jnp.float32).reshape((high - low) * local_ch, block)
        )

    def convolve(padded, zeros, toep, mixed, outgoing, low, high):
        for c in range(local_ch):
            shifted = jnp.concatenate(
                [
                    padded[pl.ds((zeros + low - d) * local_ch + c, high - low, stride=local_ch), :]
                    for d in range(high)
                ],
                axis=1,
            ).astype(jnp.bfloat16)
            mixed[pl.ds(low * local_ch + c, high - low, stride=local_ch), :] = jnp.dot(
                shifted, toep[c, : high * block, :], preferred_element_type=jnp.float32
            )
        outgoing[low:high] = (
            mixed[low * local_ch : high * local_ch, :]
            .reshape(high - low, local_ch, block)
            .astype(jnp.bfloat16)
        )

    def send_back(outgoing, slot, sent, low, high):
        def one(k, carry):
            peer = upper * (low + k) + (1 - upper) * (high - 1 - k)

            @pl.when(peer != me)
            def _():
                push(outgoing.at[peer], conv_ref.at[slot], sent, back_recv_sem, peer)

            return carry

        lax.fori_loop(0, high - low, one, 0)

    for group, (low, high) in enumerate(((0, FIRST), (FIRST, half))):
        take(arrived_ref, padded_ref, shards - 1, recv_sem.at[group], low, high)

        @pl.when((upper == 0) | alone)
        def _(low=low, high=high):
            convolve(padded_ref, shards - 1, toep_ref, mixed_ref, outgoing_ref, low, high)
            send_back(outgoing_ref, me, back_send_sem, low, high)

        @pl.when(borrows)
        def _(group=group, low=low, high=high):
            take(
                low_arrived_ref, low_padded_ref, half - 1, low_recv_sem.at[group], low, high
            )
            convolve(
                low_padded_ref, half - 1, low_toep_ref, low_mixed_ref, low_outgoing_ref, low, high
            )
            send_back(low_outgoing_ref, partner, low_back_send_sem, low, high)

    for low in range(half, shards, FIRST):
        high = low + FIRST
        take(arrived_ref, padded_ref, shards - 1, recv_sem.at[low // FIRST], low, high)
        convolve(padded_ref, shards - 1, toep_ref, mixed_ref, outgoing_ref, low, high)
        send_back(outgoing_ref, me, back_send_sem, low, high)

    pltpu.make_async_copy(outgoing_ref.at[me], conv_ref.at[me], back_recv_sem).start()

    @pl.when(borrows)
    def _():
        pltpu.make_async_copy(
            low_outgoing_ref.at[me], conv_ref.at[partner], back_recv_sem
        ).start()

    others = arrived_ref.at[pl.ds(0, shards - 1)]
    skip_load.wait()
    columns = jnp.broadcast_to(skip_ref[...][None, :], (block, shards * local_ch)).T
    skipped_ref[...] = columns * gated_ref[...].astype(jnp.float32).reshape(
        shards * local_ch, block
    )
    few = arrived_ref.at[pl.ds(0, half - 1)]
    pltpu.make_async_copy(others, others, send_sem).wait()
    pltpu.make_async_copy(conv_ref, conv_ref, back_recv_sem).wait()

    @pl.when((upper == 0) & ((tensor > 0) | (me == 0)))
    def _():
        pltpu.make_async_copy(few, few, low_send_sem).wait()

    @pl.when((upper == 0) & (tensor == 0) & (me > 0))
    def _():
        fewer = arrived_ref.at[pl.ds(0, half - 2)]
        pltpu.make_async_copy(fewer, fewer, low_send_sem).wait()

    @pl.when(borrows)
    def _():
        pltpu.make_async_copy(few, few, low_back_send_sem).wait()

    @pl.when((upper == 0) | alone)
    def _():
        pltpu.make_async_copy(others, others, back_send_sem).wait()

    @pl.when(lends)
    def _():
        pltpu.make_async_copy(lent_ref, lent_ref, lend_sem).wait()
        pltpu.make_async_copy(few, few, back_send_sem).wait()


def in_hbm(array):
    return pltpu.with_memory_space_constraint(array, pltpu.HBM)


def per_device(queries, keys, values, filters, skip):
    channels, block = keys.shape
    shards = lax.axis_size("context")
    local_ch = channels // shards
    half = shards // 2
    stacked = (shards, local_ch, block)
    vmem = pl.BlockSpec(memory_space=pltpu.VMEM)
    anywhere = pl.BlockSpec(memory_space=pltpu.HBM)
    conv, skipped = pl.pallas_call(
        conv_kernel,
        out_shape=(
            jax.ShapeDtypeStruct(stacked, jnp.bfloat16),
            jax.ShapeDtypeStruct((channels, block), jnp.float32),
        ),
        in_specs=[anywhere] * 4,
        out_specs=(vmem, vmem),
        scratch_shapes=[
            pltpu.VMEM(stacked, jnp.bfloat16),
            pltpu.VMEM((channels,), jnp.float32),
            pltpu.VMEM(stacked, jnp.bfloat16),
            pltpu.VMEM(stacked, jnp.bfloat16),
            pltpu.VMEM((local_ch, shards * block), jnp.float32),
            pltpu.VMEM((local_ch, shards * block, block), jnp.bfloat16),
            pltpu.VMEM(stacked, jnp.bfloat16),
            pltpu.VMEM(((2 * shards - 1) * local_ch, block), jnp.float32),
            pltpu.VMEM((shards * local_ch, block), jnp.float32),
            pltpu.VMEM(stacked, jnp.bfloat16),
            pltpu.VMEM((half, local_ch, block), jnp.bfloat16),
            pltpu.VMEM((half, local_ch, block), jnp.bfloat16),
            pltpu.VMEM((local_ch, half * block, block), jnp.bfloat16),
            pltpu.VMEM((half, local_ch, block), jnp.bfloat16),
            pltpu.VMEM(((2 * half - 1) * local_ch, block), jnp.float32),
            pltpu.VMEM((half * local_ch, block), jnp.float32),
            pltpu.VMEM((half, local_ch, block), jnp.bfloat16),
            pltpu.SemaphoreType.DMA((4,)),
            pltpu.SemaphoreType.DMA,
            pltpu.SemaphoreType.DMA((4,)),
            pltpu.SemaphoreType.DMA,
            pltpu.SemaphoreType.DMA((2,)),
            pltpu.SemaphoreType.DMA,
            pltpu.SemaphoreType.DMA,
            pltpu.SemaphoreType.DMA,
            pltpu.SemaphoreType.DMA,
            pltpu.SemaphoreType.DMA,
            pltpu.SemaphoreType.REGULAR,
        ],
        compiler_params=pltpu.CompilerParams(
            collective_id=0, has_side_effects=True, vmem_limit_bytes=40 << 20
        ),
        name="hyena_conv",
    )(*(in_hbm(x) for x in (keys.reshape(stacked), values.reshape(stacked), filters, skip)))
    result = queries.astype(jnp.float32) * (
        conv.reshape(channels, block).astype(jnp.float32) + skipped
    )
    return result.astype(jnp.bfloat16)


def solution(mesh):
    placed = (
        P("tensor", "context"),
        P("tensor", "context"),
        P("tensor", "context"),
        P(("tensor", "context"), None),
        P("tensor"),
    )
    return jax.shard_map(
        per_device, mesh=mesh, in_specs=placed, out_specs=P("tensor", "context"), check_vma=False
    )
```

```python
import functools

import jax
import jax.numpy as jnp
from jax import lax
from jax.experimental import pallas as pl
from jax.experimental.pallas import tpu as pltpu
from jax.sharding import PartitionSpec as P

MESH = pl.DeviceIdType.MESH
FIRST = 8
TAIL = 4


def conv_kernel(
    keys_hbm,
    values_hbm,
    filters_hbm,
    skip_hbm,
    conv_ref,
    skipped_ref,
    gated_ref,
    skip_ref,
    keys_ref,
    values_ref,
    taps_ref,
    toep_ref,
    arrived_ref,
    padded_ref,
    mixed_ref,
    outgoing_ref,
    lent_ref,
    borrowed_ref,
    low_toep_ref,
    low_arrived_ref,
    low_padded_ref,
    low_mixed_ref,
    low_outgoing_ref,
    load_sem,
    send_sem,
    recv_sem,
    low_send_sem,
    low_recv_sem,
    lend_sem,
    borrow_sem,
    back_send_sem,
    low_back_send_sem,
    back_recv_sem,
    last_sem,
):
    shards, local_ch, block = gated_ref.shape
    me = lax.axis_index("context")
    tensor = lax.axis_index("tensor")
    half = shards // 2
    upper = me // half
    partner = lax.rem(me + half, shards)
    barrier = pltpu.get_barrier_semaphore()

    first_group = 1 - lax.min(tensor, 1)
    is_last = me + tensor == 0
    alone = (tensor == 0) & (partner == 0)
    borrows = (upper == 0) & (me + tensor > 0)
    lends = (upper == 1) & (partner + tensor > 0)

    def greet(k, carry):
        peer = lax.rem(me + k, shards)
        pl.semaphore_signal(barrier, inc=1, device_id=(tensor, peer), device_id_type=MESH)
        return carry

    @pl.when(jnp.logical_not(is_last))
    def _():
        lax.fori_loop(1, shards, greet, 0)

    key_load = pltpu.make_async_copy(keys_hbm, keys_ref, load_sem.at[0])
    value_load = pltpu.make_async_copy(values_hbm, values_ref, load_sem.at[1])
    tap_load = pltpu.make_async_copy(filters_hbm, taps_ref, load_sem.at[2])
    key_load.start()
    value_load.start()
    tap_load.start()
    skip_load = pltpu.make_async_copy(skip_hbm, skip_ref, load_sem.at[3])
    skip_load.start()
    padded_ref[pl.ds(0, (shards - 1) * local_ch), :] = jnp.zeros(
        ((shards - 1) * local_ch, block), jnp.float32
    )
    low_padded_ref[pl.ds(0, (half - 1) * local_ch), :] = jnp.zeros(
        ((half - 1) * local_ch, block), jnp.float32
    )
    key_load.wait()
    value_load.wait()
    gated_ref[...] = (
        keys_ref[...].astype(jnp.float32) * values_ref[...].astype(jnp.float32)
    ).astype(jnp.bfloat16)
    tap_load.wait()
    for d in range(half):
        lent_ref[d] = taps_ref[:, d * block : (d + 1) * block].astype(jnp.bfloat16)

    row_ids = lax.broadcasted_iota(jnp.int32, (block, block), 0)
    col_ids = lax.broadcasted_iota(jnp.int32, (block, block), 1)
    same_block = col_ids >= row_ids

    def turn(row):
        return pltpu.roll(jnp.broadcast_to(row, (block, block)), 0, 1, stride=1, stride_axis=0)

    def build(row_of, into, c, first, last):
        before = turn(row_of(first - 1)) if first else jnp.zeros((block, block), jnp.float32)
        for d in range(first, last):
            turned = turn(row_of(d))
            into[c, d * block : (d + 1) * block, :] = jnp.where(
                same_block, turned, before
            ).astype(jnp.bfloat16)
            before = turned

    def build_own(c):
        def row_of(d):
            return taps_ref[c : c + 1, d * block : (d + 1) * block]

        build(row_of, toep_ref, c, 0, shards)

    def build_borrowed(first, last):
        for c in range(local_ch):

            def row_of(d, c=c):
                return borrowed_ref[d].astype(jnp.float32)[c : c + 1, :]

            build(row_of, low_toep_ref, c, first, last)

    @pl.when(borrows)
    def _():
        for c in range(local_ch):
            build_own(c)

    pl.semaphore_wait(barrier, shards - 1 - first_group * lax.min(me, 1))

    @pl.when(is_last)
    def _():
        def announce(peer, carry):
            pl.semaphore_signal(last_sem, inc=1, device_id=(tensor, peer), device_id_type=MESH)
            return carry

        lax.fori_loop(1, shards, announce, 0)


    def push(source, target, sent, received, peer):
        pltpu.make_async_remote_copy(
            src_ref=source,
            dst_ref=target,
            send_sem=sent,
            recv_sem=received,
            device_id=(tensor, peer),
            device_id_type=MESH,
        ).start()

    mine = recv_sem.at[me // TAIL]
    low_mine = low_recv_sem.at[lax.rem(me, half) // FIRST]

    def send_out(peer):
        push(gated_ref.at[peer], arrived_ref.at[me], send_sem, mine, peer)

    def send_both(peer):
        push(gated_ref.at[peer + half], low_arrived_ref.at[me], low_send_sem, low_mine, peer)
        send_out(peer)

    def lend():
        push(lent_ref, borrowed_ref, lend_sem, borrow_sem, partner)

    @pl.when(upper == 0)
    def _():
        def send_low(peer, carry):
            @pl.when((peer != me) & (peer + 1 - first_group > 0))
            def _():
                send_both(peer)

            return carry

        def send_high(k, carry):
            send_out(shards - 1 - k)
            return carry

        lax.fori_loop(0, half, send_low, 0)

        @pl.when(borrows)
        def _():
            pltpu.make_async_copy(gated_ref.at[partner], low_arrived_ref.at[me], low_mine).start()

        lax.fori_loop(0, half, send_high, 0)

    @pl.when(upper == 1)
    def _():
        @pl.when(lends)
        def _():
            lend()

        def send_any(peer, carry):
            @pl.when((peer != me) & (peer + 1 - first_group > 0))
            def _():
                send_out(peer)

            return carry

        lax.fori_loop(0, shards, send_any, 0)

    pltpu.make_async_copy(gated_ref.at[me], arrived_ref.at[me], mine).start()

    @pl.when(jnp.logical_not(borrows))
    def _():
        for c in range(local_ch):
            build_own(c)

    @pl.when((tensor == 0) & (me > 0))
    def _():
        pl.semaphore_wait(last_sem, 1)
        send_out(0)

    @pl.when(borrows)
    def _():
        pltpu.make_async_copy(borrowed_ref, borrowed_ref, borrow_sem).wait()
        build_borrowed(0, half)

    def take(arrived, padded, zeros, sem, low, high):
        part = arrived.at[low:high]
        pltpu.make_async_copy(part, part, sem).wait()
        padded[(zeros + low) * local_ch : (zeros + high) * local_ch, :] = (
            part[...].astype(jnp.float32).reshape((high - low) * local_ch, block)
        )

    def convolve(padded, zeros, toep, mixed, outgoing, low, high):
        for c in range(local_ch):
            shifted = jnp.concatenate(
                [
                    padded[pl.ds((zeros + low - d) * local_ch + c, high - low, stride=local_ch), :]
                    for d in range(high)
                ],
                axis=1,
            ).astype(jnp.bfloat16)
            mixed[pl.ds(low * local_ch + c, high - low, stride=local_ch), :] = jnp.dot(
                shifted, toep[c, : high * block, :], preferred_element_type=jnp.float32
            )
        outgoing[low:high] = (
            mixed[low * local_ch : high * local_ch, :]
            .reshape(high - low, local_ch, block)
            .astype(jnp.bfloat16)
        )

    def send_back(outgoing, slot, sent, low, high):
        def one(k, carry):
            peer = upper * (low + k) + (1 - upper) * (high - 1 - k)

            @pl.when(peer != me)
            def _():
                push(outgoing.at[peer], conv_ref.at[slot], sent, back_recv_sem, peer)

            return carry

        lax.fori_loop(0, high - low, one, 0)

    def take_own(low, high):
        for start in range(low, high, TAIL):
            take(
                arrived_ref,
                padded_ref,
                shards - 1,
                recv_sem.at[start // TAIL],
                start,
                start + TAIL,
            )

    take_own(0, half)

    @pl.when((upper == 0) | alone)
    def _():
        convolve(padded_ref, shards - 1, toep_ref, mixed_ref, outgoing_ref, 0, half)
        send_back(outgoing_ref, me, back_send_sem, 0, half)

    @pl.when(borrows)
    def _():
        for group in range(half // FIRST):
            take(
                low_arrived_ref,
                low_padded_ref,
                half - 1,
                low_recv_sem.at[group],
                group * FIRST,
                group * FIRST + FIRST,
            )
        convolve(low_padded_ref, half - 1, low_toep_ref, low_mixed_ref, low_outgoing_ref, 0, half)
        send_back(low_outgoing_ref, partner, low_back_send_sem, 0, half)

    def upper_rows(low, high):
        take_own(low, high)
        convolve(padded_ref, shards - 1, toep_ref, mixed_ref, outgoing_ref, low, high)
        send_back(outgoing_ref, me, back_send_sem, low, high)

    @pl.when(is_last)
    def _():
        edge = shards - TAIL
        for low in range(half, shards - FIRST, FIRST):
            upper_rows(low, low + FIRST)
        take_own(shards - FIRST, edge)
        padded_ref[(shards - 1 + edge) * local_ch :, :] = jnp.zeros(
            (TAIL * local_ch, block), jnp.float32
        )
        convolve(
            padded_ref, shards - 1, toep_ref, mixed_ref, outgoing_ref, shards - FIRST, shards
        )
        send_back(outgoing_ref, me, back_send_sem, shards - FIRST, edge)
        part = arrived_ref.at[edge:shards]
        pltpu.make_async_copy(part, part, recv_sem.at[edge // TAIL]).wait()
        low_padded_ref[(half - 1) * local_ch : (half - 1 + TAIL) * local_ch, :] = (
            part[...].astype(jnp.float32).reshape(TAIL * local_ch, block)
        )
        for c in range(local_ch):
            shifted = jnp.concatenate(
                [
                    low_padded_ref[pl.ds((half - 1 - d) * local_ch + c, TAIL, stride=local_ch), :]
                    for d in range(TAIL)
                ],
                axis=1,
            ).astype(jnp.bfloat16)
            rows = pl.ds(edge * local_ch + c, TAIL, stride=local_ch)
            mixed_ref[rows, :] = mixed_ref[rows, :] + jnp.dot(
                shifted, toep_ref[c, : TAIL * block, :], preferred_element_type=jnp.float32
            )
        outgoing_ref[edge:shards] = (
            mixed_ref[edge * local_ch :, :].reshape(TAIL, local_ch, block).astype(jnp.bfloat16)
        )
        send_back(outgoing_ref, me, back_send_sem, edge, shards)

    @pl.when(jnp.logical_not(is_last))
    def _():
        upper_rows(half, shards)

    pltpu.make_async_copy(outgoing_ref.at[me], conv_ref.at[me], back_recv_sem).start()

    @pl.when(borrows)
    def _():
        pltpu.make_async_copy(
            low_outgoing_ref.at[me], conv_ref.at[partner], back_recv_sem
        ).start()

    others = arrived_ref.at[pl.ds(0, shards - 1)]
    skip_load.wait()
    columns = jnp.broadcast_to(skip_ref[...][None, :], (block, shards * local_ch)).T
    skipped_ref[...] = columns * gated_ref[...].astype(jnp.float32).reshape(
        shards * local_ch, block
    )
    few = arrived_ref.at[pl.ds(0, half - 1)]
    pltpu.make_async_copy(others, others, send_sem).wait()
    pltpu.make_async_copy(conv_ref, conv_ref, back_recv_sem).wait()

    @pl.when((upper == 0) & ((tensor > 0) | (me == 0)))
    def _():
        pltpu.make_async_copy(few, few, low_send_sem).wait()

    @pl.when((upper == 0) & (tensor == 0) & (me > 0))
    def _():
        fewer = arrived_ref.at[pl.ds(0, half - 2)]
        pltpu.make_async_copy(fewer, fewer, low_send_sem).wait()

    @pl.when(borrows)
    def _():
        pltpu.make_async_copy(few, few, low_back_send_sem).wait()

    @pl.when((upper == 0) | alone)
    def _():
        pltpu.make_async_copy(others, others, back_send_sem).wait()

    @pl.when(lends)
    def _():
        pltpu.make_async_copy(lent_ref, lent_ref, lend_sem).wait()
        pltpu.make_async_copy(few, few, back_send_sem).wait()


def in_hbm(array):
    return pltpu.with_memory_space_constraint(array, pltpu.HBM)


def per_device(queries, keys, values, filters, skip):
    channels, block = keys.shape
    shards = lax.axis_size("context")
    local_ch = channels // shards
    half = shards // 2
    stacked = (shards, local_ch, block)
    vmem = pl.BlockSpec(memory_space=pltpu.VMEM)
    anywhere = pl.BlockSpec(memory_space=pltpu.HBM)
    conv, skipped = pl.pallas_call(
        conv_kernel,
        out_shape=(
            jax.ShapeDtypeStruct(stacked, jnp.bfloat16),
            jax.ShapeDtypeStruct((channels, block), jnp.float32),
        ),
        in_specs=[anywhere] * 4,
        out_specs=(vmem, vmem),
        scratch_shapes=[
            pltpu.VMEM(stacked, jnp.bfloat16),
            pltpu.VMEM((channels,), jnp.float32),
            pltpu.VMEM(stacked, jnp.bfloat16),
            pltpu.VMEM(stacked, jnp.bfloat16),
            pltpu.VMEM((local_ch, shards * block), jnp.float32),
            pltpu.VMEM((local_ch, shards * block, block), jnp.bfloat16),
            pltpu.VMEM(stacked, jnp.bfloat16),
            pltpu.VMEM(((2 * shards - 1) * local_ch, block), jnp.float32),
            pltpu.VMEM((shards * local_ch, block), jnp.float32),
            pltpu.VMEM(stacked, jnp.bfloat16),
            pltpu.VMEM((half, local_ch, block), jnp.bfloat16),
            pltpu.VMEM((half, local_ch, block), jnp.bfloat16),
            pltpu.VMEM((local_ch, half * block, block), jnp.bfloat16),
            pltpu.VMEM((half, local_ch, block), jnp.bfloat16),
            pltpu.VMEM(((2 * half - 1) * local_ch, block), jnp.float32),
            pltpu.VMEM((half * local_ch, block), jnp.float32),
            pltpu.VMEM((half, local_ch, block), jnp.bfloat16),
            pltpu.SemaphoreType.DMA((4,)),
            pltpu.SemaphoreType.DMA,
            pltpu.SemaphoreType.DMA((shards // TAIL,)),
            pltpu.SemaphoreType.DMA,
            pltpu.SemaphoreType.DMA((2,)),
            pltpu.SemaphoreType.DMA,
            pltpu.SemaphoreType.DMA,
            pltpu.SemaphoreType.DMA,
            pltpu.SemaphoreType.DMA,
            pltpu.SemaphoreType.DMA,
            pltpu.SemaphoreType.REGULAR,
        ],
        compiler_params=pltpu.CompilerParams(
            collective_id=0, has_side_effects=True, vmem_limit_bytes=40 << 20
        ),
        name="hyena_conv",
    )(*(in_hbm(x) for x in (keys.reshape(stacked), values.reshape(stacked), filters, skip)))
    result = queries.astype(jnp.float32) * (
        conv.reshape(channels, block).astype(jnp.float32) + skipped
    )
    return result.astype(jnp.bfloat16)


def solution(mesh):
    placed = (
        P("tensor", "context"),
        P("tensor", "context"),
        P("tensor", "context"),
        P(("tensor", "context"), None),
        P("tensor"),
    )
    return jax.shard_map(
        per_device, mesh=mesh, in_specs=placed, out_specs=P("tensor", "context"), check_vma=False
    )
```

```python
import functools

import jax
import jax.numpy as jnp
from jax import lax
from jax.experimental import pallas as pl
from jax.experimental.pallas import tpu as pltpu
from jax.sharding import PartitionSpec as P

MESH = pl.DeviceIdType.MESH
FIRST = 8
TAIL = 4


def conv_kernel(
    keys_hbm,
    values_hbm,
    filters_hbm,
    skip_hbm,
    conv_ref,
    skipped_ref,
    gated_ref,
    skip_ref,
    keys_ref,
    values_ref,
    taps_ref,
    toep_ref,
    arrived_ref,
    padded_ref,
    mixed_ref,
    outgoing_ref,
    lent_ref,
    borrowed_ref,
    low_toep_ref,
    low_arrived_ref,
    low_padded_ref,
    low_mixed_ref,
    low_outgoing_ref,
    load_sem,
    send_sem,
    recv_sem,
    low_send_sem,
    low_recv_sem,
    lend_sem,
    borrow_sem,
    back_send_sem,
    low_back_send_sem,
    back_recv_sem,
    last_sem,
    upper_sem,
):
    shards, local_ch, block = gated_ref.shape
    me = lax.axis_index("context")
    tensor = lax.axis_index("tensor")
    half = shards // 2
    upper = me // half
    partner = lax.rem(me + half, shards)
    barrier = pltpu.get_barrier_semaphore()

    first_group = 1 - lax.min(tensor, 1)
    is_last = me + tensor == 0
    alone = (tensor == 0) & (partner == 0)
    borrows = (upper == 0) & (me + tensor > 0)
    lends = (upper == 1) & (partner + tensor > 0)

    staged = 1 - lax.min(lax.rem(tensor // 2, 4) // 2, 1)

    def greet(k, carry):
        peer = lax.rem(me + k, shards)

        @pl.when((upper * staged == 0) | (peer >= half) | (peer + tensor == 0))
        def _():
            pl.semaphore_signal(barrier, inc=1, device_id=(tensor, peer), device_id_type=MESH)

        return carry

    @pl.when(jnp.logical_not(is_last))
    def _():
        lax.fori_loop(1, shards, greet, 0)

    key_load = pltpu.make_async_copy(keys_hbm, keys_ref, load_sem.at[0])
    value_load = pltpu.make_async_copy(values_hbm, values_ref, load_sem.at[1])
    tap_load = pltpu.make_async_copy(filters_hbm, taps_ref, load_sem.at[2])
    key_load.start()
    value_load.start()
    tap_load.start()
    skip_load = pltpu.make_async_copy(skip_hbm, skip_ref, load_sem.at[3])
    skip_load.start()
    padded_ref[pl.ds(0, (shards - 1) * local_ch), :] = jnp.zeros(
        ((shards - 1) * local_ch, block), jnp.float32
    )
    low_padded_ref[pl.ds(0, (half - 1) * local_ch), :] = jnp.zeros(
        ((half - 1) * local_ch, block), jnp.float32
    )
    key_load.wait()
    value_load.wait()
    gated_ref[...] = (
        keys_ref[...].astype(jnp.float32) * values_ref[...].astype(jnp.float32)
    ).astype(jnp.bfloat16)
    tap_load.wait()
    for d in range(half):
        lent_ref[d] = taps_ref[:, d * block : (d + 1) * block].astype(jnp.bfloat16)

    row_ids = lax.broadcasted_iota(jnp.int32, (block, block), 0)
    col_ids = lax.broadcasted_iota(jnp.int32, (block, block), 1)
    same_block = col_ids >= row_ids

    def turn(row):
        return pltpu.roll(jnp.broadcast_to(row, (block, block)), 0, 1, stride=1, stride_axis=0)

    def build(row_of, into, c, first, last):
        before = turn(row_of(first - 1)) if first else jnp.zeros((block, block), jnp.float32)
        for d in range(first, last):
            turned = turn(row_of(d))
            into[c, d * block : (d + 1) * block, :] = jnp.where(
                same_block, turned, before
            ).astype(jnp.bfloat16)
            before = turned

    def build_own(c):
        def row_of(d):
            return taps_ref[c : c + 1, d * block : (d + 1) * block]

        build(row_of, toep_ref, c, 0, shards)

    def build_borrowed(first, last):
        for c in range(local_ch):

            def row_of(d, c=c):
                return borrowed_ref[d].astype(jnp.float32)[c : c + 1, :]

            build(row_of, low_toep_ref, c, first, last)

    @pl.when(borrows)
    def _():
        for c in range(local_ch):
            build_own(c)

    hidden = staged * (1 - upper) * lax.min(me + tensor, 1) * half
    pl.semaphore_wait(barrier, shards - 1 - first_group * lax.min(me, 1) - hidden)

    @pl.when(upper * staged == 1)
    def _():
        def arise(peer, carry):
            pl.semaphore_signal(upper_sem, inc=1, device_id=(tensor, peer), device_id_type=MESH)
            return carry

        lax.fori_loop(first_group, half, arise, 0)

    @pl.when(is_last)
    def _():
        def announce(peer, carry):
            pl.semaphore_signal(last_sem, inc=1, device_id=(tensor, peer), device_id_type=MESH)
            return carry

        lax.fori_loop(1, shards, announce, 0)


    def push(source, target, sent, received, peer):
        pltpu.make_async_remote_copy(
            src_ref=source,
            dst_ref=target,
            send_sem=sent,
            recv_sem=received,
            device_id=(tensor, peer),
            device_id_type=MESH,
        ).start()

    mine = recv_sem.at[me // TAIL]
    low_mine = low_recv_sem.at[lax.rem(me, half) // FIRST]

    def send_out(peer):
        push(gated_ref.at[peer], arrived_ref.at[me], send_sem, mine, peer)

    def send_both(peer):
        push(gated_ref.at[peer + half], low_arrived_ref.at[me], low_send_sem, low_mine, peer)
        send_out(peer)

    def lend():
        push(lent_ref, borrowed_ref, lend_sem, borrow_sem, partner)

    @pl.when(upper == 0)
    def _():
        def send_low(peer, carry):
            @pl.when((peer != me) & (peer + 1 - first_group > 0))
            def _():
                send_both(peer)

            return carry

        def send_high(k, carry):
            send_out(shards - 1 - k)
            return carry

        lax.fori_loop(0, half, send_low, 0)

        @pl.when(borrows)
        def _():
            pltpu.make_async_copy(gated_ref.at[partner], low_arrived_ref.at[me], low_mine).start()

        @pl.when(hidden > 0)
        def _():
            pl.semaphore_wait(upper_sem, half)

        lax.fori_loop(0, half, send_high, 0)

    @pl.when(upper == 1)
    def _():
        @pl.when(lends)
        def _():
            lend()

        def send_any(peer, carry):
            @pl.when((peer != me) & (peer + 1 - first_group > 0))
            def _():
                send_out(peer)

            return carry

        lax.fori_loop(0, shards, send_any, 0)

    pltpu.make_async_copy(gated_ref.at[me], arrived_ref.at[me], mine).start()

    @pl.when(jnp.logical_not(borrows))
    def _():
        for c in range(local_ch):
            build_own(c)

    @pl.when((tensor == 0) & (me > 0))
    def _():
        pl.semaphore_wait(last_sem, 1)
        send_out(0)

    @pl.when(borrows)
    def _():
        pltpu.make_async_copy(borrowed_ref, borrowed_ref, borrow_sem).wait()
        build_borrowed(0, half)

    def take(arrived, padded, zeros, sem, low, high):
        part = arrived.at[low:high]
        pltpu.make_async_copy(part, part, sem).wait()
        padded[(zeros + low) * local_ch : (zeros + high) * local_ch, :] = (
            part[...].astype(jnp.float32).reshape((high - low) * local_ch, block)
        )

    def convolve(padded, zeros, toep, mixed, outgoing, low, high):
        for c in range(local_ch):
            shifted = jnp.concatenate(
                [
                    padded[pl.ds((zeros + low - d) * local_ch + c, high - low, stride=local_ch), :]
                    for d in range(high)
                ],
                axis=1,
            ).astype(jnp.bfloat16)
            mixed[pl.ds(low * local_ch + c, high - low, stride=local_ch), :] = jnp.dot(
                shifted, toep[c, : high * block, :], preferred_element_type=jnp.float32
            )
        outgoing[low:high] = (
            mixed[low * local_ch : high * local_ch, :]
            .reshape(high - low, local_ch, block)
            .astype(jnp.bfloat16)
        )

    def send_back(outgoing, slot, sent, low, high):
        def one(k, carry):
            peer = upper * (low + k) + (1 - upper) * (high - 1 - k)

            @pl.when(peer != me)
            def _():
                push(outgoing.at[peer], conv_ref.at[slot], sent, back_recv_sem, peer)

            return carry

        lax.fori_loop(0, high - low, one, 0)

    def take_own(low, high):
        for start in range(low, high, TAIL):
            take(
                arrived_ref,
                padded_ref,
                shards - 1,
                recv_sem.at[start // TAIL],
                start,
                start + TAIL,
            )

    take_own(0, half)

    @pl.when((upper == 0) | alone)
    def _():
        convolve(padded_ref, shards - 1, toep_ref, mixed_ref, outgoing_ref, 0, half)
        send_back(outgoing_ref, me, back_send_sem, 0, half)

    @pl.when(borrows)
    def _():
        for group in range(half // FIRST):
            take(
                low_arrived_ref,
                low_padded_ref,
                half - 1,
                low_recv_sem.at[group],
                group * FIRST,
                group * FIRST + FIRST,
            )
        convolve(low_padded_ref, half - 1, low_toep_ref, low_mixed_ref, low_outgoing_ref, 0, half)
        send_back(low_outgoing_ref, partner, low_back_send_sem, 0, half)

    def upper_rows(low, high):
        take_own(low, high)
        convolve(padded_ref, shards - 1, toep_ref, mixed_ref, outgoing_ref, low, high)
        send_back(outgoing_ref, me, back_send_sem, low, high)

    @pl.when(is_last)
    def _():
        edge = shards - TAIL
        for low in range(half, shards - FIRST, FIRST):
            upper_rows(low, low + FIRST)
        take_own(shards - FIRST, edge)
        padded_ref[(shards - 1 + edge) * local_ch :, :] = jnp.zeros(
            (TAIL * local_ch, block), jnp.float32
        )
        convolve(
            padded_ref, shards - 1, toep_ref, mixed_ref, outgoing_ref, shards - FIRST, shards
        )
        send_back(outgoing_ref, me, back_send_sem, shards - FIRST, edge)
        part = arrived_ref.at[edge:shards]
        pltpu.make_async_copy(part, part, recv_sem.at[edge // TAIL]).wait()
        low_padded_ref[(half - 1) * local_ch : (half - 1 + TAIL) * local_ch, :] = (
            part[...].astype(jnp.float32).reshape(TAIL * local_ch, block)
        )
        for c in range(local_ch):
            shifted = jnp.concatenate(
                [
                    low_padded_ref[pl.ds((half - 1 - d) * local_ch + c, TAIL, stride=local_ch), :]
                    for d in range(TAIL)
                ],
                axis=1,
            ).astype(jnp.bfloat16)
            rows = pl.ds(edge * local_ch + c, TAIL, stride=local_ch)
            mixed_ref[rows, :] = mixed_ref[rows, :] + jnp.dot(
                shifted, toep_ref[c, : TAIL * block, :], preferred_element_type=jnp.float32
            )
        outgoing_ref[edge:shards] = (
            mixed_ref[edge * local_ch :, :].reshape(TAIL, local_ch, block).astype(jnp.bfloat16)
        )
        send_back(outgoing_ref, me, back_send_sem, edge, shards)

    @pl.when(jnp.logical_not(is_last))
    def _():
        upper_rows(half, shards)

    pltpu.make_async_copy(outgoing_ref.at[me], conv_ref.at[me], back_recv_sem).start()

    @pl.when(borrows)
    def _():
        pltpu.make_async_copy(
            low_outgoing_ref.at[me], conv_ref.at[partner], back_recv_sem
        ).start()

    others = arrived_ref.at[pl.ds(0, shards - 1)]
    skip_load.wait()
    columns = jnp.broadcast_to(skip_ref[...][None, :], (block, shards * local_ch)).T
    skipped_ref[...] = columns * gated_ref[...].astype(jnp.float32).reshape(
        shards * local_ch, block
    )
    few = arrived_ref.at[pl.ds(0, half - 1)]
    pltpu.make_async_copy(others, others, send_sem).wait()
    pltpu.make_async_copy(conv_ref, conv_ref, back_recv_sem).wait()

    @pl.when((upper == 0) & ((tensor > 0) | (me == 0)))
    def _():
        pltpu.make_async_copy(few, few, low_send_sem).wait()

    @pl.when((upper == 0) & (tensor == 0) & (me > 0))
    def _():
        fewer = arrived_ref.at[pl.ds(0, half - 2)]
        pltpu.make_async_copy(fewer, fewer, low_send_sem).wait()

    @pl.when(borrows)
    def _():
        pltpu.make_async_copy(few, few, low_back_send_sem).wait()

    @pl.when((upper == 0) | alone)
    def _():
        pltpu.make_async_copy(others, others, back_send_sem).wait()

    @pl.when(lends)
    def _():
        pltpu.make_async_copy(lent_ref, lent_ref, lend_sem).wait()
        pltpu.make_async_copy(few, few, back_send_sem).wait()


def in_hbm(array):
    return pltpu.with_memory_space_constraint(array, pltpu.HBM)


def per_device(queries, keys, values, filters, skip):
    channels, block = keys.shape
    shards = lax.axis_size("context")
    local_ch = channels // shards
    half = shards // 2
    stacked = (shards, local_ch, block)
    vmem = pl.BlockSpec(memory_space=pltpu.VMEM)
    anywhere = pl.BlockSpec(memory_space=pltpu.HBM)
    conv, skipped = pl.pallas_call(
        conv_kernel,
        out_shape=(
            jax.ShapeDtypeStruct(stacked, jnp.bfloat16),
            jax.ShapeDtypeStruct((channels, block), jnp.float32),
        ),
        in_specs=[anywhere] * 4,
        out_specs=(vmem, vmem),
        scratch_shapes=[
            pltpu.VMEM(stacked, jnp.bfloat16),
            pltpu.VMEM((channels,), jnp.float32),
            pltpu.VMEM(stacked, jnp.bfloat16),
            pltpu.VMEM(stacked, jnp.bfloat16),
            pltpu.VMEM((local_ch, shards * block), jnp.float32),
            pltpu.VMEM((local_ch, shards * block, block), jnp.bfloat16),
            pltpu.VMEM(stacked, jnp.bfloat16),
            pltpu.VMEM(((2 * shards - 1) * local_ch, block), jnp.float32),
            pltpu.VMEM((shards * local_ch, block), jnp.float32),
            pltpu.VMEM(stacked, jnp.bfloat16),
            pltpu.VMEM((half, local_ch, block), jnp.bfloat16),
            pltpu.VMEM((half, local_ch, block), jnp.bfloat16),
            pltpu.VMEM((local_ch, half * block, block), jnp.bfloat16),
            pltpu.VMEM((half, local_ch, block), jnp.bfloat16),
            pltpu.VMEM(((2 * half - 1) * local_ch, block), jnp.float32),
            pltpu.VMEM((half * local_ch, block), jnp.float32),
            pltpu.VMEM((half, local_ch, block), jnp.bfloat16),
            pltpu.SemaphoreType.DMA((4,)),
            pltpu.SemaphoreType.DMA,
            pltpu.SemaphoreType.DMA((shards // TAIL,)),
            pltpu.SemaphoreType.DMA,
            pltpu.SemaphoreType.DMA((2,)),
            pltpu.SemaphoreType.DMA,
            pltpu.SemaphoreType.DMA,
            pltpu.SemaphoreType.DMA,
            pltpu.SemaphoreType.DMA,
            pltpu.SemaphoreType.DMA,
            pltpu.SemaphoreType.REGULAR,
            pltpu.SemaphoreType.REGULAR,
        ],
        compiler_params=pltpu.CompilerParams(
            collective_id=0, has_side_effects=True, vmem_limit_bytes=40 << 20
        ),
        name="hyena_conv",
    )(*(in_hbm(x) for x in (keys.reshape(stacked), values.reshape(stacked), filters, skip)))
    result = queries.astype(jnp.float32) * (
        conv.reshape(channels, block).astype(jnp.float32) + skipped
    )
    return result.astype(jnp.bfloat16)


def solution(mesh):
    placed = (
        P("tensor", "context"),
        P("tensor", "context"),
        P("tensor", "context"),
        P(("tensor", "context"), None),
        P("tensor"),
    )
    return jax.shard_map(
        per_device, mesh=mesh, in_specs=placed, out_specs=P("tensor", "context"), check_vma=False
    )
```
